128 devices in a mesh: row: 16 (over z, y), col: 8 (over x, core).
Axes of the slice: x: 4, y: 4, z: 4, core: 2. Of those that a mesh axis runs over, the one named last changes fastest.
Arguments:
- tiles: bfloat16 [1024, 64, 128, 128], P('row', 'col'), may hold values from -0.0625 to 0.0625
- tile_cols: int32 [1024, 64], P('row', 'col'), may hold values from 0 to 63
- counts: int32 [1024, 8], P('row', 'col'), may hold values from 1 to 8
- scales: float32 [1024, 64], P('row', 'col'), may hold values from 0.5 to 6
- sketch: bfloat16 [65536, 256], P('col'), may hold values from -6 to 6
Outputs:
- basis: float32 [131072, 256], P(('row', 'col'))
- r_factor: float32 [256, 256], replicated
The draws below stay inside these ranges and needn't reach their ends.
All inputs are finite; a program needn't handle non-finite values.
Results may differ from the reference program's by a relative error of at most 0.0029.
Values sent between devices are 32-bit elements; how exact they have to be, the bound alone decides.
No kernel may reach another device: no remote copies, remote signals or barrier semaphores. Data moves between devices by JAX's collectives and lax.ppermute only.
A program may use at most 192 MiB of HBM per device.

```python
import jax
import jax.numpy as jnp
from jax import lax

TILE = 128
K = 256
SLOTS = 8
CB_DEV = 64
NRB = 1024
ROWS = 131072
SLOTS_ALL = 64
NCB = 512


def draw_counts(key, part):
    groups_count = SLOTS_ALL // SLOTS
    values = jax.random.randint(jax.random.fold_in(key, 11), (NRB, groups_count), 1, SLOTS + 1)
    values = values.at[0, :].set(SLOTS)
    values = values.at[1, :].set(1)
    return values.astype(jnp.int32)


def draw_scales(key, part):
    inner = jax.random.fold_in(key, 23)
    ramp = 1.0 + 2.0 * jnp.arange(NRB, dtype=jnp.float32) / max(NRB - 1, 1)
    base = jnp.exp(jax.random.uniform(inner, (NRB, SLOTS_ALL), jnp.float32, jnp.log(0.5), jnp.log(2.0)))
    return (base * ramp[:, None]).astype(jnp.float32)


def touch_ends(array, own_key, least, top_value):
    spot = [jax.random.randint(jax.random.fold_in(own_key, axis), (), 0, length) for axis, length in enumerate(array.shape)]
    main_axis = array.shape.index(max(array.shape))
    neighbour = spot[:main_axis] + [(spot[main_axis] + 1) % array.shape[main_axis]] + spot[main_axis + 1:]
    return array.at[tuple(spot)].set(least).at[tuple(neighbour)].set(top_value)


def shard_levels(key, dims, split, smallest, top_value):
    def one(axis_at, parts):
        steps = jax.random.uniform(jax.random.fold_in(jax.random.fold_in(key, 6), axis_at), (parts,), jnp.float32, smallest / len(split), top_value / len(split))
        return jnp.repeat(jnp.exp(steps), dims[axis_at] // parts).reshape((-1,) + (1,) * (len(dims) - axis_at - 1))

    level = one(*split[0])
    for cut in split[1:]:
        level = level * one(*cut)
    return level


def normal_values(rng, extent, deviation, most, pieces=(), held_as=jnp.bfloat16):
    entries = deviation * jax.random.normal(rng, extent, jnp.float32)
    if pieces:
        entries = entries * shard_levels(rng, extent, pieces, -0.22, 0.18)
    return jnp.clip(entries, -most, most).astype(held_as)


def setup_inputs(seed: int = 0) -> dict:
    seeds = jax.random.split(jax.random.key(seed), 6)
    tiles = normal_values(seeds[0], (NRB, SLOTS_ALL, TILE, TILE), (TILE * SLOTS_ALL) ** -0.5, 0.0625, ((0, 16), (1, 8)))
    tile_cols = touch_ends(jax.random.randint(seeds[1], (NRB, SLOTS_ALL), 0, CB_DEV), jax.random.fold_in(seeds[1], 1), 0, CB_DEV - 1).astype(jnp.int32)
    counts = draw_counts(jax.random.fold_in(seeds[5], 71), 0)
    scales = draw_scales(jax.random.fold_in(seeds[5], 71), 0)
    sketch = normal_values(seeds[4], (NCB * TILE, K), 1.0, 6.0, ((0, 8),))
    return {"tiles": tiles, "tile_cols": tile_cols, "counts": counts, "scales": scales, "sketch": sketch}


def reference(tiles, tile_cols, counts, scales, sketch):
    groups_count = SLOTS_ALL // SLOTS
    sketch_blocks = sketch.reshape(NCB, TILE, K)
    slot_index = jnp.arange(SLOTS_ALL, dtype=jnp.int32)
    groups = slot_index // SLOTS

    def one_row(inputs):
        row_tiles, row_cols, row_scales, row_counts = inputs
        live_mask = slot_index % SLOTS < row_counts[groups]
        eff_scale = jnp.where(live_mask, row_scales, 0.0)
        dense = (row_tiles.astype(jnp.float32) * eff_scale[:, None, None]).astype(jnp.bfloat16)
        blocks = sketch_blocks[groups * CB_DEV + row_cols]
        dense = dense.astype(jnp.float32).reshape(groups_count, SLOTS, TILE, TILE)
        blocks = blocks.astype(jnp.float32).reshape(groups_count, SLOTS, TILE, K)
        partial_value = jnp.einsum('csij,csjk->cik', dense, blocks)
        return lax.optimization_barrier(jnp.sum(partial_value, axis=0))
    product = lax.map(one_row, (tiles, tile_cols, scales, counts))
    product = product.reshape(ROWS, K)
    gram = jnp.dot(product.T.astype(jnp.float32), product.astype(jnp.float32), precision=lax.Precision.HIGHEST, preferred_element_type=jnp.float32)
    lower_factor = jnp.linalg.cholesky(gram)
    solved = lax.linalg.triangular_solve(lower_factor, product, left_side=False, lower=True, transpose_a=True)
    root = jnp.sqrt(jnp.float32(ROWS))
    return (solved * root, lower_factor.T / root)
```

```python
import functools

import jax
import jax.numpy as jnp
from jax import lax
from jax.experimental import pallas as pl
from jax.experimental.pallas import tpu as pltpu
from jax.sharding import PartitionSpec as P

F32 = jnp.float32
BF16 = jnp.bfloat16
RB = 4
SLOTS = 8
T = 128
K = 256
HALF = RB * T


def split(a):
    hi = a.astype(BF16)
    return hi, (a - hi.astype(F32)).astype(BF16)


def dot(a, b, dims=((1,), (0,))):
    return lax.dot_general(a, b, (dims, ((), ())), preferred_element_type=F32)


def dot3(a, b, dims=((1,), (0,))):
    ah, al = split(a)
    bh, bl = split(b)
    return dot(ah, bh, dims) + (dot(ah, bl, dims) + dot(al, bh, dims))


def spmm_kernel(extra, two_out, hg, cols, counts, scales, tiles, sketch, *refs):
    adds = refs[:extra]
    outs = refs[extra:]
    step = pl.program_id(0)
    base = hg[step] * RB
    for r in range(RB):
        row = base + r
        live = counts[row]
        dense = []
        blocks = []
        for s in range(SLOTS):
            scale = jnp.where(s < live, scales[row * SLOTS + s], 0.0)
            dense.append((tiles[r, s].astype(F32) * scale).astype(BF16))
            start = pl.multiple_of(cols[row * SLOTS + s] * T, T)
            blocks.append(sketch[pl.ds(start, T), :])
        acc = dot(jnp.concatenate(dense, axis=1), jnp.concatenate(blocks, axis=0))
        rows = slice(r * T, (r + 1) * T)
        if extra >= 1:
            acc = acc + adds[0][0, rows, :]
        if not two_out:
            outs[0][0, rows, :] = acc
        else:
            for h in range(2):
                @pl.when(step == h)
                def _():
                    if extra == 3:
                        outs[h][rows, :] = acc + adds[1 + h][rows, :]
                    else:
                        outs[h][rows, :] = acc


def spmm(hg, meta, tiles, sketch, adds=(), two_out=False):
    cols, counts, scales = meta
    whole = pl.BlockSpec((HALF, K), lambda i, *_: (0, 0))
    part = pl.BlockSpec((1, HALF, K), lambda i, *_: (i, 0, 0))
    in_specs = [
        pl.BlockSpec((RB, SLOTS, T, T), lambda i, hg, *_: (hg[i], 0, 0, 0)),
        pl.BlockSpec(sketch.shape, lambda i, *_: (0, 0), pipeline_mode=pl.Buffered(1)),
    ]
    in_specs += [part if a.ndim == 3 else whole for a in adds]
    if two_out:
        out_shape = [jax.ShapeDtypeStruct((HALF, K), F32)] * 2
        out_specs = [whole] * 2
    else:
        out_shape = jax.ShapeDtypeStruct((2, HALF, K), F32)
        out_specs = part
    return pl.pallas_call(
        functools.partial(spmm_kernel, len(adds), two_out),
        grid_spec=pltpu.PrefetchScalarGridSpec(
            num_scalar_prefetch=4, grid=(2,), in_specs=in_specs, out_specs=out_specs
        ),
        out_shape=out_shape,
        cost_estimate=pl.CostEstimate(
            flops=2 * 2 * HALF * SLOTS * T * K, bytes_accessed=8 << 20, transcendentals=0
        ),
        name="spmm",
    )(hg, cols, counts, scales, tiles, sketch, *adds)


PACK = 272
PH = PACK // 2


def gram_kernel(core, s_ref, vp, um, up, vm, prod, keep, send, acc, pack):
    chunk = 256
    for j in range(1024 // chunk):
        h, o = divmod(j * chunk, HALF)
        rows = slice(o, o + chunk)
        first, second = ((vp, um), (up, vm))[h]
        p = s_ref[h, rows, :] + (first[rows, :] + second[rows, :])
        prod[j * chunk:(j + 1) * chunk, :] = p
        hi, lo = split(p)
        main = dot(hi, hi, ((0,), (0,)))
        cross = dot(hi, lo, ((0,), (0,)))
        if j == 0:
            acc[0] = main
            acc[1] = cross
        else:
            acc[0] += main
            acc[1] += cross
    g = acc[0] + (acc[1] + acc[1].T)
    low = g[T:, T:]
    r = lax.broadcasted_iota(jnp.int32, (T, T), 0)
    c = lax.broadcasted_iota(jnp.int32, (T, T), 1)
    pack[0:T, :] = jnp.where(r >= c, g[:T, :T], low)
    pack[T:K, :] = g[T:, :T]
    diag = jnp.sum(jnp.where(r == c, low, 0.0), axis=0, keepdims=True)
    pack[K:PACK, :] = jnp.broadcast_to(diag, (PACK - K, T))

    @pl.when(core[0] == 0)
    def _():
        keep[...] = pack[:PH, :]
        send[...] = pack[PH:, :]

    @pl.when(core[0] != 0)
    def _():
        keep[...] = pack[PH:, :]
        send[...] = pack[:PH, :]


def gram(core, s, vp, um, up, vm):
    half = pl.BlockSpec((HALF, K), lambda i, *_: (0, 0))
    return pl.pallas_call(
        gram_kernel,
        grid_spec=pltpu.PrefetchScalarGridSpec(
            num_scalar_prefetch=1,
            grid=(1,),
            in_specs=[pl.BlockSpec((2, HALF, K), lambda i, *_: (0, 0, 0))] + [half] * 4,
            out_specs=[pl.BlockSpec((2 * HALF, K), lambda i, *_: (0, 0))]
            + [pl.BlockSpec((PH, T), lambda i, *_: (0, 0))] * 2,
            scratch_shapes=[pltpu.VMEM((2, K, K), F32), pltpu.VMEM((PACK, T), F32)],
        ),
        out_shape=[jax.ShapeDtypeStruct((2 * HALF, K), F32)]
        + [jax.ShapeDtypeStruct((PH, T), F32)] * 2,
        name="gram",
    )(core, s, vp, um, up, vm)


def basis_kernel(root, core, mine, other, prod, basis, rfac, pack, a_ref, w_ref, e_ref):
    @pl.when(core[0] == 0)
    def _():
        pack[:PH, :] = mine[...]
        pack[PH:, :] = other[...]

    @pl.when(core[0] != 0)
    def _():
        pack[:PH, :] = other[...]
        pack[PH:, :] = mine[...]

    r = lax.broadcasted_iota(jnp.int32, (T, T), 0)
    c = lax.broadcasted_iota(jnp.int32, (T, T), 1)
    m = pack[0:T, :]
    mt = m.T
    b = pack[T:K, :]
    a_ref[:T, :T] = jnp.where(r >= c, m, mt)
    a_ref[T:, :T] = b
    a_ref[:T, T:] = b.T
    a_ref[T:, T:] = jnp.where(r < c, m, jnp.where(r > c, mt, pack[K:K + 1, :]))

    rr = lax.broadcasted_iota(jnp.int32, (K, K), 0)
    cc = lax.broadcasted_iota(jnp.int32, (K, K), 1)
    eye = rr == cc
    a = a_ref[...]
    masked = jnp.where(eye, a, 0.0)
    dcol = lax.rsqrt(jnp.sum(masked, axis=1, keepdims=True))
    drow = lax.rsqrt(jnp.sum(masked, axis=0, keepdims=True))
    unit = jnp.where(eye, 0.0, a * dcol * drow)
    e_ref[...] = unit
    w_ref[...] = jnp.where(eye, 1.0, 0.0)

    def size(e):
        return jnp.max(jnp.sum(jnp.abs(e), axis=0, keepdims=True))

    def update(e):
        phi = jnp.where(rr > cc, e, jnp.where(eye, 0.5 * e, 0.0)).astype(BF16)
        w = w_ref[...]
        t = dot(phi, w.astype(BF16))
        w_ref[...] = w - t + dot(phi, t.astype(BF16))

    def cond(state):
        it, err = state
        return jnp.logical_and(err >= 0.01, it < 10)

    def body(state):
        it, _ = state
        update(e_ref[...])
        w = w_ref[...]
        scaled = jnp.where(eye, 1.0, unit)
        t = dot3(w, scaled)
        e = dot3(t, w, ((1,), (1,))) - jnp.where(eye, 1.0, 0.0)
        e_ref[...] = e
        return it + 1, size(e)

    _, err = lax.while_loop(cond, body, (jnp.int32(0), size(unit)))
    good = err < 0.01

    @pl.when(good)
    def _():
        update(e_ref[...])
        w_ref[...] = w_ref[...] * drow

    @pl.when(jnp.logical_not(good))
    def _():
        w_ref[...] = jnp.where(eye, 1.0, 0.0)
        e_ref[...] = a_ref[...]
        lane = lax.broadcasted_iota(jnp.int32, (1, K), 1)

        def step(k, carry):
            arow = e_ref[pl.ds(k, 1), :]
            wrow = w_ref[pl.ds(k, 1), :]
            inv = lax.rsqrt(jnp.sum(jnp.where(lane == k, arow, 0.0), axis=1, keepdims=True))
            arow = arow * inv
            wrow = wrow * inv
            full = e_ref[...]
            col = jnp.sum(jnp.where(cc == k, full, 0.0), axis=1, keepdims=True) * inv
            col = jnp.where(rr[:, :1] > k, col, 0.0)
            e_ref[...] = full - col * arow
            w_ref[...] = w_ref[...] - col * wrow
            w_ref[pl.ds(k, 1), :] = wrow
            return carry

        lax.fori_loop(0, K, step, 0)

    w = w_ref[...]
    upper = dot3(w, a_ref[...])
    rfac[...] = jnp.where(rr <= cc, upper, 0.0) * (1.0 / root)
    wh, wl = split(w * root)
    for j in range(4):
        rows = slice(j * 256, (j + 1) * 256)
        ph, plo = split(prod[rows, :])
        dims = ((1,), (1,))
        basis[rows, :] = dot(ph, wh, dims) + (dot(ph, wl, dims) + dot(plo, wh, dims))


def finish(root, core, mine, other, prod):
    def full(*shape):
        return pl.BlockSpec(shape, lambda i, *_: (0,) * len(shape))

    return pl.pallas_call(
        functools.partial(basis_kernel, root),
        grid_spec=pltpu.PrefetchScalarGridSpec(
            num_scalar_prefetch=1,
            grid=(1,),
            in_specs=[full(PH, T), full(PH, T), full(2 * HALF, K)],
            out_specs=[full(2 * HALF, K), full(K, K)],
            scratch_shapes=[pltpu.VMEM((PACK, T), F32)] + [pltpu.VMEM((K, K), F32)] * 3,
        ),
        out_shape=[
            jax.ShapeDtypeStruct((2 * HALF, K), F32),
            jax.ShapeDtypeStruct((K, K), F32),
        ],
        name="finish",
    )(core, mine, other, prod)


def perm(size, target):
    return [(i, target(i)) for i in range(size)]


def on_device(tiles, tile_cols, counts, scales, sketch):
    rows_all = tiles.shape[0] * T * lax.axis_size("row")
    me = lax.axis_index("col")
    x, core = me // 2, me % 2
    meta = (tile_cols.reshape(-1), counts.reshape(-1), scales.reshape(-1))

    partner = perm(8, lambda c: c ^ 1)
    plus = perm(8, lambda c: (c + 2) % 8)
    minus = perm(8, lambda c: (c + 6) % 8)

    def ids(*items):
        return jnp.stack([((x + dx) % 4 * 2 + a) * 2 + h for dx, a, h in items]).astype(jnp.int32)

    other = 1 - core
    sp = functools.partial(spmm, meta=meta, tiles=tiles, sketch=sketch)

    q = sp(ids((2, other, 0), (2, other, 1)))
    c1 = lax.ppermute(q, "col", partner)
    d2p, d2m = sp(ids((2, core, 0), (2, core, 1)), adds=(c1,), two_out=True)
    tp = lax.ppermute(d2p, "col", plus)
    tm = lax.ppermute(d2m, "col", minus)
    q = sp(ids((1, other, 1), (3, other, 0)))
    c2 = lax.ppermute(q, "col", partner)
    up, um = sp(ids((1, core, 1), (3, core, 0)), adds=(c2,), two_out=True)
    up = lax.ppermute(up, "col", plus)
    um = lax.ppermute(um, "col", minus)
    q = sp(ids((1, other, 0), (3, other, 1)))
    c3 = lax.ppermute(q, "col", partner)
    vp, vm = sp(ids((1, core, 0), (3, core, 1)), adds=(c3, tp, tm), two_out=True)
    vp = lax.ppermute(vp, "col", plus)
    vm = lax.ppermute(vm, "col", minus)
    q = sp(ids((0, other, 0), (0, other, 1)))
    c4 = lax.ppermute(q, "col", partner)
    s = sp(ids((0, core, 0), (0, core, 1)), adds=(c4,))

    which = core.reshape(1).astype(jnp.int32)
    prod, keep, send = gram(which, s, vp, um, up, vm)
    tot = keep + lax.ppermute(send, "col", partner)
    even = lambda v: v ^ 1
    odd = lambda v: (v + (1 if v % 2 else 3)) % 4
    for pair in (even, odd):
        tot = tot + lax.ppermute(tot, "col", perm(8, lambda c: pair(c // 2) * 2 + c % 2))
        tot = tot + lax.ppermute(tot, "row", perm(16, lambda r: r // 4 * 4 + pair(r % 4)))
        tot = tot + lax.ppermute(tot, "row", perm(16, lambda r: pair(r // 4) * 4 + r % 4))
    rest = lax.ppermute(tot, "col", partner)
    basis, rfac = finish(float(rows_all) ** 0.5, which, tot, rest, prod)
    return basis, rfac


def solution(mesh):
    in_specs = (
        P("row", "col", None, None),
        P("row", "col"),
        P("row", "col"),
        P("row", "col"),
        P("col", None),
    )
    out_specs = (P(("row", "col"), None), P())
    return jax.shard_map(
        on_device, mesh=mesh, in_specs=in_specs, out_specs=out_specs, check_vma=False
    )
```

```python
import functools

import jax
import jax.numpy as jnp
from jax import lax
from jax.experimental import pallas as pl
from jax.experimental.pallas import tpu as pltpu
from jax.sharding import PartitionSpec as P


F32 = jnp.float32
BF16 = jnp.bfloat16
RB = 4
SLOTS = 8
T = 128
K = 256
HALF = RB * T
VMEM_LIMIT = 16 << 20
SKETCH_PIECES = 16


def split(a):
    hi = a.astype(BF16)
    return hi, (a - hi.astype(F32)).astype(BF16)


def dot(a, b, dims=((1,), (0,))):
    return lax.dot_general(a, b, (dims, ((), ())), preferred_element_type=F32)


def dot3(a, b, dims=((1,), (0,))):
    ah, al = split(a)
    bh, bl = split(b)
    return dot(ah, bh, dims) + (dot(ah, bl, dims) + dot(al, bh, dims))


def first_row(item):
    dx, flip, half = item
    me = lax.axis_index("col")
    return ((((me >> 1) + dx) & 3) * 2 + ((me + flip) & 1)) * 2 * RB + half * RB


def block_row(row, tile, cols, counts, scales, sketch):
    live = counts[0, row]
    dense = []
    blocks = []
    for s in range(SLOTS):
        scale = jnp.where(s < live, scales[s, row], 0.0)
        dense.append((tile(s).astype(F32) * scale).astype(BF16))
        start = pl.multiple_of(cols[s, row] * T, T)
        blocks.append(sketch[pl.ds(start, T), :])
    return dot(jnp.concatenate(dense, axis=1), jnp.concatenate(blocks, axis=0))


def first_kernel(items, kept, cols, counts, scales, tiles, sketch, *refs):
    n = len(items)
    outs, (held, local), (tile_sem, held_sem, sketch_sem) = refs[:n], refs[n:n + 2], refs[n + 3:]
    buf = refs[n + 2]
    piece = local.shape[0] // SKETCH_PIECES
    load = []
    for j in range(SKETCH_PIECES):
        rows = pl.ds(j * piece, piece)
        load.append(pltpu.make_async_copy(sketch.at[rows], local.at[rows], sketch_sem.at[j]))
    tile_load, held_load = [], []
    for group, into, sem, out in ((items, buf, tile_sem, tile_load), (kept, held, held_sem, held_load)):
        for i, item in enumerate(group):
            for r in range(RB):
                for p in range(2):
                    part = pl.ds(p * (SLOTS // 2), SLOTS // 2)
                    to = i * RB + r
                    out.append(pltpu.make_async_copy(
                        tiles.at[first_row(item) + r, part], into.at[to, part], sem.at[2 * to + p]
                    ))
    for copy in load + tile_load + held_load:
        copy.start()
    for copy in load:
        copy.wait()
    for i, item in enumerate(items):
        for r in range(RB):
            to = i * RB + r
            tile_load[2 * to].wait()
            tile_load[2 * to + 1].wait()
            outs[i][r * T:(r + 1) * T, :] = block_row(
                first_row(item) + r, lambda s: buf[to, s], cols, counts, scales, local
            )
    for copy in held_load:
        copy.wait()


def first(items, kept, meta, tiles, sketch):
    vmem = pl.BlockSpec(memory_space=pltpu.VMEM)
    smem = pl.BlockSpec(memory_space=pltpu.SMEM)
    hbm = pl.BlockSpec(memory_space=pltpu.HBM)
    rows, keep = RB * len(items), RB * len(kept)
    return pl.pallas_call(
        functools.partial(first_kernel, items, kept),
        in_specs=[smem] * 3 + [hbm] * 2,
        out_specs=[vmem] * (len(items) + 2),
        out_shape=[jax.ShapeDtypeStruct((HALF, K), F32)] * len(items)
        + [
            jax.ShapeDtypeStruct((keep, SLOTS, T, T), BF16),
            jax.ShapeDtypeStruct(sketch.shape, BF16),
        ],
        scratch_shapes=[
            pltpu.VMEM((rows, SLOTS, T, T), BF16),
            pltpu.SemaphoreType.DMA((2 * rows,)),
            pltpu.SemaphoreType.DMA((2 * keep,)),
            pltpu.SemaphoreType.DMA((SKETCH_PIECES,)),
        ],
        compiler_params=pltpu.CompilerParams(vmem_limit_bytes=VMEM_LIMIT),
        cost_estimate=pl.CostEstimate(
            flops=2 * len(items) * HALF * SLOTS * T * K, bytes_accessed=8 << 20, transcendentals=0
        ),
        name="first",
    )(*meta, tiles, sketch)


def spmm_kernel(items, joins, waits, held, cols, counts, scales, tiles, sketch, *refs):
    adds = refs[:joins]
    outs = refs[joins + waits:]
    for n, item in enumerate(items):
        base = first_row(item)
        for r in range(RB):
            at = held * RB + n * RB + r if held is not None else base + r
            acc = block_row(base + r, lambda s: tiles[at, s], cols, counts, scales, sketch)
            rows = slice(r * T, (r + 1) * T)
            for j in range(n, joins, len(items)):
                acc = acc + adds[j][rows, :]
            outs[n][rows, :] = acc


def spmm(items, meta, tiles, sketch, adds=(), after=(), held=None):
    vmem = pl.BlockSpec(memory_space=pltpu.VMEM)
    smem = pl.BlockSpec(memory_space=pltpu.SMEM)
    anywhere = pl.BlockSpec(memory_space=pl.ANY)
    return pl.pallas_call(
        functools.partial(spmm_kernel, items, len(adds), len(after), held),
        in_specs=[smem] * 3 + [vmem] * (2 + len(adds)) + [anywhere] * len(after),
        out_specs=[vmem] * len(items),
        out_shape=[jax.ShapeDtypeStruct((HALF, K), F32)] * len(items),
        compiler_params=pltpu.CompilerParams(vmem_limit_bytes=VMEM_LIMIT),
        cost_estimate=pl.CostEstimate(
            flops=2 * len(items) * HALF * SLOTS * T * K, bytes_accessed=4 << 20, transcendentals=0
        ),
        name="spmm",
    )(*meta, tiles, sketch, *adds, *after)


PACK = 272
PH = PACK // 2


def gram_kernel(s0, s1, vp, um, up, vm, prod, keep, send, acc, pack):
    chunk = 256
    core = lax.axis_index("col") & 1
    for j in range(1024 // chunk):
        h, o = divmod(j * chunk, HALF)
        rows = slice(o, o + chunk)
        first, second = ((vp, um), (up, vm))[h]
        p = (s0, s1)[h][rows, :] + (first[rows, :] + second[rows, :])
        prod[j * chunk:(j + 1) * chunk, :] = p
        hi, lo = split(p)
        main = dot(hi, hi, ((0,), (0,)))
        cross = dot(hi, lo, ((0,), (0,)))
        if j == 0:
            acc[0] = main
            acc[1] = cross
        else:
            acc[0] += main
            acc[1] += cross
    g = acc[0] + (acc[1] + acc[1].T)
    low = g[T:, T:]
    r = lax.broadcasted_iota(jnp.int32, (T, T), 0)
    c = lax.broadcasted_iota(jnp.int32, (T, T), 1)
    pack[0:T, :] = jnp.where(r >= c, g[:T, :T], low)
    pack[T:K, :] = g[T:, :T]
    diag = jnp.sum(jnp.where(r == c, low, 0.0), axis=0, keepdims=True)
    pack[K:PACK, :] = jnp.broadcast_to(diag, (PACK - K, T))

    @pl.when(core == 0)
    def _():
        keep[...] = pack[:PH, :]
        send[...] = pack[PH:, :]

    @pl.when(core == 1)
    def _():
        keep[...] = pack[PH:, :]
        send[...] = pack[:PH, :]


def gram(s0, s1, vp, um, up, vm):
    vmem = pl.BlockSpec(memory_space=pltpu.VMEM)
    return pl.pallas_call(
        gram_kernel,
        in_specs=[vmem] * 6,
        out_specs=[vmem] * 3,
        scratch_shapes=[pltpu.VMEM((2, K, K), F32), pltpu.VMEM((PACK, T), F32)],
        out_shape=[jax.ShapeDtypeStruct((2 * HALF, K), F32)]
        + [jax.ShapeDtypeStruct((PH, T), F32)] * 2,
        compiler_params=pltpu.CompilerParams(vmem_limit_bytes=VMEM_LIMIT),
        name="gram",
    )(s0, s1, vp, um, up, vm)


def basis_kernel(root, mine, other, prod, basis, rfac, pack, a_ref, w_ref, e_ref):
    core = lax.axis_index("col") & 1

    @pl.when(core == 0)
    def _():
        pack[:PH, :] = mine[...]
        pack[PH:, :] = other[...]

    @pl.when(core == 1)
    def _():
        pack[:PH, :] = other[...]
        pack[PH:, :] = mine[...]

    r = lax.broadcasted_iota(jnp.int32, (T, T), 0)
    c = lax.broadcasted_iota(jnp.int32, (T, T), 1)
    m = pack[0:T, :]
    mt = m.T
    b = pack[T:K, :]
    a_ref[:T, :T] = jnp.where(r >= c, m, mt)
    a_ref[T:, :T] = b
    a_ref[:T, T:] = b.T
    a_ref[T:, T:] = jnp.where(r < c, m, jnp.where(r > c, mt, pack[K:K + 1, :]))

    rr = lax.broadcasted_iota(jnp.int32, (K, K), 0)
    cc = lax.broadcasted_iota(jnp.int32, (K, K), 1)
    eye = rr == cc
    a = a_ref[...]
    masked = jnp.where(eye, a, 0.0)
    dcol = lax.rsqrt(jnp.sum(masked, axis=1, keepdims=True))
    drow = lax.rsqrt(jnp.sum(masked, axis=0, keepdims=True))
    unit = jnp.where(eye, 0.0, a * dcol * drow)
    e_ref[...] = unit
    w_ref[...] = jnp.where(eye, 1.0, 0.0)

    def size(e):
        return jnp.max(jnp.sum(jnp.abs(e), axis=0, keepdims=True))

    def update(e):
        phi = jnp.where(rr > cc, e, jnp.where(eye, 0.5 * e, 0.0)).astype(BF16)
        w = w_ref[...]
        t = dot(phi, w.astype(BF16))
        w_ref[...] = w - t + dot(phi, t.astype(BF16))

    def cond(state):
        it, err = state
        return jnp.logical_and(err >= 0.01, it < 10)

    def body(state):
        it, _ = state
        update(e_ref[...])
        w = w_ref[...]
        scaled = jnp.where(eye, 1.0, unit)
        t = dot3(w, scaled)
        e = dot3(t, w, ((1,), (1,))) - jnp.where(eye, 1.0, 0.0)
        e_ref[...] = e
        return it + 1, size(e)

    _, err = lax.while_loop(cond, body, (jnp.int32(0), size(unit)))
    good = err < 0.01

    @pl.when(good)
    def _():
        update(e_ref[...])
        w_ref[...] = w_ref[...] * drow

    @pl.when(jnp.logical_not(good))
    def _():
        w_ref[...] = jnp.where(eye, 1.0, 0.0)
        e_ref[...] = a_ref[...]
        lane = lax.broadcasted_iota(jnp.int32, (1, K), 1)

        def step(k, carry):
            arow = e_ref[pl.ds(k, 1), :]
            wrow = w_ref[pl.ds(k, 1), :]
            inv = lax.rsqrt(jnp.sum(jnp.where(lane == k, arow, 0.0), axis=1, keepdims=True))
            arow = arow * inv
            wrow = wrow * inv
            full = e_ref[...]
            col = jnp.sum(jnp.where(cc == k, full, 0.0), axis=1, keepdims=True) * inv
            col = jnp.where(rr[:, :1] > k, col, 0.0)
            e_ref[...] = full - col * arow
            w_ref[...] = w_ref[...] - col * wrow
            w_ref[pl.ds(k, 1), :] = wrow
            return carry

        lax.fori_loop(0, K, step, 0)

    w = w_ref[...]
    upper = dot3(w, a_ref[...])
    rfac[...] = jnp.where(rr <= cc, upper, 0.0) * (1.0 / root)
    wh, wl = split(w * root)
    for j in range(4):
        rows = slice(j * 256, (j + 1) * 256)
        ph, plo = split(prod[rows, :])
        dims = ((1,), (1,))
        basis[rows, :] = dot(ph, wh, dims) + (dot(ph, wl, dims) + dot(plo, wh, dims))


def finish(root, mine, other, prod):
    vmem = pl.BlockSpec(memory_space=pltpu.VMEM)
    return pl.pallas_call(
        functools.partial(basis_kernel, root),
        in_specs=[vmem] * 3,
        out_specs=[vmem] * 2,
        scratch_shapes=[pltpu.VMEM((PACK, T), F32)] + [pltpu.VMEM((K, K), F32)] * 3,
        out_shape=[
            jax.ShapeDtypeStruct((2 * HALF, K), F32),
            jax.ShapeDtypeStruct((K, K), F32),
        ],
        compiler_params=pltpu.CompilerParams(vmem_limit_bytes=VMEM_LIMIT),
        name="finish",
    )(mine, other, prod)


def perm(size, target):
    return [(i, target(i)) for i in range(size)]


def on_device(tiles, tile_cols, counts, scales, sketch):
    rows_all = tiles.shape[0] * T * lax.axis_size("row")
    meta = tuple(
        pltpu.with_memory_space_constraint(a, pltpu.HBM) for a in (tile_cols.T, counts.T, scales.T)
    )
    partner = perm(8, lambda c: c ^ 1)
    plus = perm(8, lambda c: (c + 2) % 8)
    minus = perm(8, lambda c: (c + 6) % 8)

    def move(q, to):
        return lax.ppermute(q, "col", to)

    qa, qb, held, local = first(
        ((2, 1, 0), (2, 1, 1)),
        ((2, 0, 0), (2, 0, 1)),
        meta,
        pltpu.with_memory_space_constraint(tiles, pltpu.HBM),
        pltpu.with_memory_space_constraint(sketch, pltpu.HBM),
    )
    later, _ = lax.optimization_barrier((tiles, qa))
    near = pltpu.with_memory_space_constraint(later, pltpu.VMEM)

    def sp(*items, tiles=near, **kw):
        return spmm(items, meta, tiles, local, **kw)

    ca, cb = move(qa, partner), move(qb, partner)
    (d2p,) = sp((2, 0, 0), tiles=held, held=0, adds=(ca,))
    tp = move(d2p, plus)
    (d2m,) = sp((2, 0, 1), tiles=held, held=1, adds=(cb,), after=(d2p,))
    tm = move(d2m, minus)
    qu = sp((1, 1, 1), (3, 1, 0), after=(d2m,))
    cu = [move(q, partner) for q in qu]
    qv = sp((1, 1, 0), (3, 1, 1), after=qu)
    cv = [move(q, partner) for q in qv]
    up, um = sp((1, 0, 1), (3, 0, 0), adds=cu, after=qv)
    mid = up
    up, um = move(up, plus), move(um, minus)
    qo = sp((0, 1, 0), (0, 1, 1), after=(mid,))
    co = [move(q, partner) for q in qo]
    vp, vm = sp((1, 0, 0), (3, 0, 1), adds=(*cv, tp, tm), after=qo)
    last = vp
    vp, vm = move(vp, plus), move(vm, minus)
    s0, s1 = sp((0, 0, 0), (0, 0, 1), adds=co, after=(last,))

    prod, keep, send = gram(s0, s1, vp, um, up, vm)
    tot = keep + move(send, partner)
    even = lambda v: v ^ 1
    odd = lambda v: (v + (1 if v % 2 else 3)) % 4
    for pair in (even, odd):
        tot = tot + lax.ppermute(tot, "col", perm(8, lambda c: pair(c // 2) * 2 + c % 2))
        tot = tot + lax.ppermute(tot, "row", perm(16, lambda r: r // 4 * 4 + pair(r % 4)))
        tot = tot + lax.ppermute(tot, "row", perm(16, lambda r: pair(r // 4) * 4 + r % 4))
    rest = move(tot, partner)
    basis, rfac = finish(float(rows_all) ** 0.5, tot, rest, prod)
    return basis, rfac


def solution(mesh):
    in_specs = (
        P("row", "col", None, None),
        P("row", "col"),
        P("row", "col"),
        P("row", "col"),
        P("col", None),
    )
    out_specs = (P(("row", "col"), None), P())

    return jax.shard_map(
        on_device, mesh=mesh, in_specs=in_specs, out_specs=out_specs, check_vma=False
    )
```

```python
import functools

import jax
import jax.numpy as jnp
from jax import lax
from jax.experimental import pallas as pl
from jax.experimental.pallas import tpu as pltpu
from jax.sharding import PartitionSpec as P


F32 = jnp.float32
BF16 = jnp.bfloat16
RB = 4
SLOTS = 8
T = 128
K = 256
HALF = RB * T
VMEM_LIMIT = 16 << 20
SKETCH_PIECES = 16


def split(a):
    hi = a.astype(BF16)
    return hi, (a - hi.astype(F32)).astype(BF16)


def dot(a, b, dims=((1,), (0,))):
    return lax.dot_general(a, b, (dims, ((), ())), preferred_element_type=F32)


def dot3(a, b, dims=((1,), (0,))):
    ah, al = split(a)
    bh, bl = split(b)
    return dot(ah, bh, dims) + (dot(ah, bl, dims) + dot(al, bh, dims))


def first_row(me, item):
    dx, flip, half = item
    return ((((me >> 1) + dx) & 3) * 2 + ((me + flip) & 1)) * 2 * RB + half * RB


def block_row(row, tile, cols, counts, scales, sketch):
    live = counts[0, row]
    dense = []
    blocks = []
    for s in range(SLOTS):
        scaled = jnp.where(s < live, tile(s).astype(F32) * scales[s, row], 0.0)
        dense.append(scaled.astype(BF16))
        start = pl.multiple_of(cols[s, row] * T, T)
        blocks.append(sketch[pl.ds(start, T), :])
    return dot(jnp.concatenate(dense, axis=1), jnp.concatenate(blocks, axis=0))


def tile_copies(me, items, counts, tiles, into, sem):
    copies = []
    for i, item in enumerate(items):
        for r in range(RB):
            row = first_row(me, item) + r
            pairs = (counts[0, row] + 1) >> 1
            at = i * RB + r
            for p in range(1, SLOTS // 2 + 1):
                part = pl.ds(0, 2 * p)
                copy = pltpu.make_async_copy(tiles.at[row, part], into.at[at, part], sem.at[at])
                copies.append((pairs == p, copy))
    return copies


def start_all(copies):
    for chosen, copy in copies:
        pl.when(chosen)(copy.start)


def wait_all(copies):
    for chosen, copy in copies:
        pl.when(chosen)(copy.wait)


def first_kernel(items, kept, cols, counts, scales, tiles, sketch, *refs):
    n = len(items)
    outs, (held, local) = refs[:n], refs[n:n + 2]
    buf, meta, meta_sem, tile_sem, held_sem, sketch_sem = (
        refs[n + 2], refs[n + 3:n + 6], *refs[n + 6:]
    )
    me = lax.axis_index("col")
    piece = local.shape[0] // SKETCH_PIECES
    load = [
        pltpu.make_async_copy(src, dst, meta_sem.at[i])
        for i, (src, dst) in enumerate(zip((cols, counts, scales), meta))
    ]
    for j in range(SKETCH_PIECES):
        rows = pl.ds(j * piece, piece)
        load.append(pltpu.make_async_copy(sketch.at[rows], local.at[rows], sketch_sem.at[j]))
    for copy in load:
        copy.start()
    for copy in load[:3]:
        copy.wait()
    mine = tile_copies(me, items, meta[1], tiles, buf, tile_sem)
    later = tile_copies(me, kept, meta[1], tiles, held, held_sem)
    start_all(mine)
    start_all(later)
    for copy in load[3:]:
        copy.wait()
    wait_all(mine)
    for i, item in enumerate(items):
        base = first_row(me, item)
        for r in range(RB):
            outs[i][r * T:(r + 1) * T, :] = block_row(
                base + r, lambda s: buf[i * RB + r, s], *meta, local
            )
    wait_all(later)


def first(items, kept, meta, tiles, sketch):
    vmem = pl.BlockSpec(memory_space=pltpu.VMEM)
    hbm = pl.BlockSpec(memory_space=pltpu.HBM)
    rows, keep = RB * len(items), RB * len(kept)
    return pl.pallas_call(
        functools.partial(first_kernel, items, kept),
        in_specs=[hbm] * 5,
        out_specs=[vmem] * (len(items) + 2),
        out_shape=[jax.ShapeDtypeStruct((HALF, K), F32)] * len(items)
        + [
            jax.ShapeDtypeStruct((keep, SLOTS, T, T), BF16),
            jax.ShapeDtypeStruct(sketch.shape, BF16),
        ],
        scratch_shapes=[pltpu.VMEM((rows, SLOTS, T, T), BF16)]
        + [pltpu.SMEM(a.shape, a.dtype) for a in meta]
        + [
            pltpu.SemaphoreType.DMA((3,)),
            pltpu.SemaphoreType.DMA((rows,)),
            pltpu.SemaphoreType.DMA((keep,)),
            pltpu.SemaphoreType.DMA((SKETCH_PIECES,)),
        ],
        compiler_params=pltpu.CompilerParams(vmem_limit_bytes=VMEM_LIMIT),
        cost_estimate=pl.CostEstimate(
            flops=2 * len(items) * HALF * SLOTS * T * K, bytes_accessed=8 << 20, transcendentals=0
        ),
        name="first",
    )(*meta, tiles, sketch)


def spmm_kernel(items, at, loads, joins, cols, counts, scales, tiles, sketch, *refs):
    n = len(items)
    me = lax.axis_index("col")
    adds, outs = refs[:joins], refs[joins:joins + n]
    held, copies = tiles, []
    if loads:
        held, sem = refs[joins + n:]
        copies = tile_copies(me, loads, counts, tiles, held, sem)
    start_all(copies)
    first_ones = RB * n * (SLOTS // 2)
    wait_all(copies[:first_ones])
    for i, item in enumerate(items):
        base = first_row(me, item)
        for r in range(RB):
            to = (at + i) * RB + r
            acc = block_row(base + r, lambda s: held[to, s], cols, counts, scales, sketch)
            rows = slice(r * T, (r + 1) * T)
            for j in range(i, joins, n):
                acc = acc + adds[j][rows, :]
            outs[i][rows, :] = acc
    wait_all(copies[first_ones:])


def spmm(items, at, meta, tiles, sketch, adds=(), loads=()):
    vmem = pl.BlockSpec(memory_space=pltpu.VMEM)
    smem = pl.BlockSpec(memory_space=pltpu.SMEM)
    hbm = pl.BlockSpec(memory_space=pltpu.HBM)
    keep = RB * len(loads)
    out_shape = [jax.ShapeDtypeStruct((HALF, K), F32)] * len(items)
    scratch = []
    if loads:
        out_shape.append(jax.ShapeDtypeStruct((keep, SLOTS, T, T), BF16))
        scratch.append(pltpu.SemaphoreType.DMA((keep,)))
    return pl.pallas_call(
        functools.partial(spmm_kernel, items, at, loads, len(adds)),
        in_specs=[smem] * 3 + [hbm if loads else vmem, vmem] + [vmem] * len(adds),
        out_specs=[vmem] * len(out_shape),
        out_shape=out_shape,
        scratch_shapes=scratch,
        compiler_params=pltpu.CompilerParams(vmem_limit_bytes=VMEM_LIMIT),
        cost_estimate=pl.CostEstimate(
            flops=2 * len(items) * HALF * SLOTS * T * K, bytes_accessed=4 << 20, transcendentals=0
        ),
        name="spmm",
    )(*meta, tiles, sketch, *adds)


PACK = 272
PH = PACK // 2


def gram_kernel(s0, s1, vp, um, up, vm, prod, keep, send, acc, pack):
    chunk = 256
    core = lax.axis_index("col") & 1
    for j in range(1024 // chunk):
        h, o = divmod(j * chunk, HALF)
        rows = slice(o, o + chunk)
        first, second = ((vp, um), (up, vm))[h]
        p = (s0, s1)[h][rows, :] + (first[rows, :] + second[rows, :])
        prod[j * chunk:(j + 1) * chunk, :] = p
        hi, lo = split(p)
        main = dot(hi, hi, ((0,), (0,)))
        cross = dot(hi, lo, ((0,), (0,)))
        if j == 0:
            acc[0] = main
            acc[1] = cross
        else:
            acc[0] += main
            acc[1] += cross
    g = acc[0] + (acc[1] + acc[1].T)
    low = g[T:, T:]
    r = lax.broadcasted_iota(jnp.int32, (T, T), 0)
    c = lax.broadcasted_iota(jnp.int32, (T, T), 1)
    pack[0:T, :] = jnp.where(r >= c, g[:T, :T], low)
    pack[T:K, :] = g[T:, :T]
    diag = jnp.sum(jnp.where(r == c, low, 0.0), axis=0, keepdims=True)
    pack[K:PACK, :] = jnp.broadcast_to(diag, (PACK - K, T))

    @pl.when(core == 0)
    def _():
        keep[...] = pack[:PH, :]
        send[...] = pack[PH:, :]

    @pl.when(core == 1)
    def _():
        keep[...] = pack[PH:, :]
        send[...] = pack[:PH, :]


def gram(s0, s1, vp, um, up, vm):
    vmem = pl.BlockSpec(memory_space=pltpu.VMEM)
    return pl.pallas_call(
        gram_kernel,
        in_specs=[vmem] * 6,
        out_specs=[vmem] * 3,
        scratch_shapes=[pltpu.VMEM((2, K, K), F32), pltpu.VMEM((PACK, T), F32)],
        out_shape=[jax.ShapeDtypeStruct((2 * HALF, K), F32)]
        + [jax.ShapeDtypeStruct((PH, T), F32)] * 2,
        compiler_params=pltpu.CompilerParams(vmem_limit_bytes=VMEM_LIMIT),
        name="gram",
    )(s0, s1, vp, um, up, vm)


def basis_kernel(root, mine, other, prod, basis, rfac, pack, a_ref, w_ref, e_ref):
    core = lax.axis_index("col") & 1

    @pl.when(core == 0)
    def _():
        pack[:PH, :] = mine[...]
        pack[PH:, :] = other[...]

    @pl.when(core == 1)
    def _():
        pack[:PH, :] = other[...]
        pack[PH:, :] = mine[...]

    r = lax.broadcasted_iota(jnp.int32, (T, T), 0)
    c = lax.broadcasted_iota(jnp.int32, (T, T), 1)
    m = pack[0:T, :]
    mt = m.T
    b = pack[T:K, :]
    a_ref[:T, :T] = jnp.where(r >= c, m, mt)
    a_ref[T:, :T] = b
    a_ref[:T, T:] = b.T
    a_ref[T:, T:] = jnp.where(r < c, m, jnp.where(r > c, mt, pack[K:K + 1, :]))

    rr = lax.broadcasted_iota(jnp.int32, (K, K), 0)
    cc = lax.broadcasted_iota(jnp.int32, (K, K), 1)
    eye = rr == cc
    a = a_ref[...]
    masked = jnp.where(eye, a, 0.0)
    dcol = lax.rsqrt(jnp.sum(masked, axis=1, keepdims=True))
    drow = lax.rsqrt(jnp.sum(masked, axis=0, keepdims=True))
    unit = jnp.where(eye, 0.0, a * dcol * drow)
    e_ref[...] = unit
    w_ref[...] = jnp.where(eye, 1.0, 0.0)

    def size(e):
        return jnp.max(jnp.sum(jnp.abs(e), axis=0, keepdims=True))

    def update(e):
        phi = jnp.where(rr > cc, e, jnp.where(eye, 0.5 * e, 0.0)).astype(BF16)
        w = w_ref[...]
        t = dot(phi, w.astype(BF16))
        w_ref[...] = w - t + dot(phi, t.astype(BF16))

    def cond(state):
        it, err = state
        return jnp.logical_and(err >= 0.01, it < 10)

    def body(state):
        it, _ = state
        update(e_ref[...])
        w = w_ref[...]
        scaled = jnp.where(eye, 1.0, unit)
        t = dot3(w, scaled)
        e = dot3(t, w, ((1,), (1,))) - jnp.where(eye, 1.0, 0.0)
        e_ref[...] = e
        return it + 1, size(e)

    _, err = lax.while_loop(cond, body, (jnp.int32(0), size(unit)))
    good = err < 0.01

    @pl.when(good)
    def _():
        update(e_ref[...])
        w_ref[...] = w_ref[...] * drow

    @pl.when(jnp.logical_not(good))
    def _():
        w_ref[...] = jnp.where(eye, 1.0, 0.0)
        e_ref[...] = a_ref[...]
        lane = lax.broadcasted_iota(jnp.int32, (1, K), 1)

        def step(k, carry):
            arow = e_ref[pl.ds(k, 1), :]
            wrow = w_ref[pl.ds(k, 1), :]
            inv = lax.rsqrt(jnp.sum(jnp.where(lane == k, arow, 0.0), axis=1, keepdims=True))
            arow = arow * inv
            wrow = wrow * inv
            full = e_ref[...]
            col = jnp.sum(jnp.where(cc == k, full, 0.0), axis=1, keepdims=True) * inv
            col = jnp.where(rr[:, :1] > k, col, 0.0)
            e_ref[...] = full - col * arow
            w_ref[...] = w_ref[...] - col * wrow
            w_ref[pl.ds(k, 1), :] = wrow
            return carry

        lax.fori_loop(0, K, step, 0)

    w = w_ref[...]
    upper = dot3(w, a_ref[...])
    rfac[...] = jnp.where(rr <= cc, upper, 0.0) * (1.0 / root)
    wh, wl = split(w * root)
    for j in range(4):
        rows = slice(j * 256, (j + 1) * 256)
        ph, plo = split(prod[rows, :])
        dims = ((1,), (1,))
        basis[rows, :] = dot(ph, wh, dims) + (dot(ph, wl, dims) + dot(plo, wh, dims))


def finish(root, mine, other, prod):
    vmem = pl.BlockSpec(memory_space=pltpu.VMEM)
    return pl.pallas_call(
        functools.partial(basis_kernel, root),
        in_specs=[vmem] * 3,
        out_specs=[vmem] * 2,
        scratch_shapes=[pltpu.VMEM((PACK, T), F32)] + [pltpu.VMEM((K, K), F32)] * 3,
        out_shape=[
            jax.ShapeDtypeStruct((2 * HALF, K), F32),
            jax.ShapeDtypeStruct((K, K), F32),
        ],
        compiler_params=pltpu.CompilerParams(vmem_limit_bytes=VMEM_LIMIT),
        name="finish",
    )(mine, other, prod)


ORDERS = ((2, 1), (1, 0), (0, 2))


def perm(size, target):
    return [(i, target(i)) for i in range(size)]


def axis_perm(order, by):
    def target(i):
        place = [i >> 5, (i >> 3) & 3, (i >> 1) & 3]
        axis = order[i & 1]
        place[axis] = (place[axis] + by) & 3
        return (((place[0] * 4 + place[1]) * 4 + place[2]) << 1) | (i & 1)

    return perm(128, target)


def on_device(tiles, tile_cols, counts, scales, sketch):
    rows_all = tiles.shape[0] * T * lax.axis_size("row")
    meta = tuple(
        pltpu.with_memory_space_constraint(a, pltpu.HBM) for a in (tile_cols.T, counts.T, scales.T)
    )
    partner = perm(8, lambda c: c ^ 1)
    plus = perm(8, lambda c: (c + 2) % 8)
    minus = perm(8, lambda c: (c + 6) % 8)

    def move(q, to):
        return lax.ppermute(q, "col", to)

    far_other = (2, 1, 0), (2, 1, 1)
    far_own = (2, 0, 0), (2, 0, 1)
    u_other, u_own = ((1, 1, 1), (3, 1, 0)), ((1, 0, 1), (3, 0, 0))
    v_other, v_own = ((1, 1, 0), (3, 1, 1)), ((1, 0, 0), (3, 0, 1))
    here_other, here_own = ((0, 1, 0), (0, 1, 1)), ((0, 0, 0), (0, 0, 1))
    tiles = pltpu.with_memory_space_constraint(tiles, pltpu.HBM)
    sketch = pltpu.with_memory_space_constraint(sketch, pltpu.HBM)

    qa, qb, held, local = first(far_other, far_own, meta, tiles, sketch)

    def sp(items, at, held, **kw):
        return spmm(items, at, meta, held, local, **kw)

    ca, cb = move(qa, partner), move(qb, partner)
    d2p, d2m = sp(far_own, 0, held, adds=(ca, cb))
    tp, tm = move(d2p, plus), move(d2m, minus)
    rest = u_other + v_other + u_own + here_other + v_own + here_own
    *qu, held = sp(u_other, 0, tiles, loads=rest)
    cu = [move(q, partner) for q in qu]
    qv = sp(v_other, 2, held)
    cv = [move(q, partner) for q in qv]
    up, um = sp(u_own, 4, held, adds=cu)
    up, um = move(up, plus), move(um, minus)
    qo = sp(here_other, 6, held)
    co = [move(q, partner) for q in qo]
    vp, vm = sp(v_own, 8, held, adds=(*cv, tp, tm))
    vp, vm = move(vp, plus), move(vm, minus)
    s0, s1 = sp(here_own, 10, held, adds=co)

    prod, keep, send = gram(s0, s1, vp, um, up, vm)
    tot = keep + move(send, partner)
    both = ("row", "col")
    for order in ORDERS:
        got = [lax.ppermute(tot, both, axis_perm(order, by)) for by in (2, 3, 1)]
        tot = (tot + got[0]) + (got[1] + got[2])
    rest = move(tot, partner)
    basis, rfac = finish(float(rows_all) ** 0.5, tot, rest, prod)
    return basis, rfac


def solution(mesh):
    in_specs = (
        P("row", "col", None, None),
        P("row", "col"),
        P("row", "col"),
        P("row", "col"),
        P("col", None),
    )
    out_specs = (P(("row", "col"), None), P())

    return jax.shard_map(
        on_device, mesh=mesh, in_specs=in_specs, out_specs=out_specs, check_vma=False
    )
```

```python
import functools

import jax
import jax.numpy as jnp
from jax import lax
from jax.experimental import pallas as pl
from jax.experimental.pallas import tpu as pltpu
from jax.sharding import PartitionSpec as P


F32 = jnp.float32
BF16 = jnp.bfloat16
RB = 4
SLOTS = 8
T = 128
K = 256
HALF = RB * T
VMEM_LIMIT = 16 << 20
SKETCH_PIECES = 16
CLOSE = 2e-3


def split(a):
    hi = a.astype(BF16)
    return hi, (a - hi.astype(F32)).astype(BF16)


def dot(a, b, dims=((1,), (0,))):
    return lax.dot_general(a, b, (dims, ((), ())), preferred_element_type=F32)


def dot3(a, b, dims=((1,), (0,))):
    ah, al = split(a)
    bh, bl = split(b)
    return dot(ah, bh, dims) + (dot(ah, bl, dims) + dot(al, bh, dims))


def first_row(me, item):
    dx, flip, half = item
    return ((((me >> 1) + dx) & 3) * 2 + ((me + flip) & 1)) * 2 * RB + half * RB


def block_row(row, tile, cols, counts, scales, sketch):
    live = counts[0, row]
    dense = []
    blocks = []
    for s in range(SLOTS):
        scaled = jnp.where(s < live, tile(s).astype(F32) * scales[s, row], 0.0)
        dense.append(scaled.astype(BF16))
        start = pl.multiple_of(cols[s, row] * T, T)
        blocks.append(sketch[pl.ds(start, T), :])
    return dot(jnp.concatenate(dense, axis=1), jnp.concatenate(blocks, axis=0))


def tile_copies(me, items, counts, tiles, into, sem):
    copies = []
    for i, item in enumerate(items):
        for r in range(RB):
            row = first_row(me, item) + r
            pairs = (counts[0, row] + 1) >> 1
            at = i * RB + r
            for p in range(1, SLOTS // 2 + 1):
                part = pl.ds(0, 2 * p)
                copy = pltpu.make_async_copy(tiles.at[row, part], into.at[at, part], sem.at[at])
                copies.append((pairs == p, copy))
    return copies


def start_all(copies):
    for chosen, copy in copies:
        pl.when(chosen)(copy.start)


def wait_all(copies):
    for chosen, copy in copies:
        pl.when(chosen)(copy.wait)


def first_kernel(items, kept, cols, counts, scales, tiles, sketch, *refs):
    n = len(items)
    outs, (held, local) = refs[:n], refs[n:n + 2]
    buf, meta, meta_sem, tile_sem, held_sem, sketch_sem = (
        refs[n + 2], refs[n + 3:n + 6], *refs[n + 6:]
    )
    me = lax.axis_index("col")
    piece = local.shape[0] // SKETCH_PIECES
    load = [
        pltpu.make_async_copy(src, dst, meta_sem.at[i])
        for i, (src, dst) in enumerate(zip((cols, counts, scales), meta))
    ]
    for j in range(SKETCH_PIECES):
        rows = pl.ds(j * piece, piece)
        load.append(pltpu.make_async_copy(sketch.at[rows], local.at[rows], sketch_sem.at[j]))
    for copy in load:
        copy.start()
    for copy in load[:3]:
        copy.wait()
    mine = tile_copies(me, items, meta[1], tiles, buf, tile_sem)
    later = tile_copies(me, kept, meta[1], tiles, held, held_sem)
    start_all(mine)
    start_all(later)
    for copy in load[3:]:
        copy.wait()
    wait_all(mine)
    for i, item in enumerate(items):
        base = first_row(me, item)
        for r in range(RB):
            outs[i][r * T:(r + 1) * T, :] = block_row(
                base + r, lambda s: buf[i * RB + r, s], *meta, local
            )
    wait_all(later)


def first(items, kept, meta, tiles, sketch):
    vmem = pl.BlockSpec(memory_space=pltpu.VMEM)
    hbm = pl.BlockSpec(memory_space=pltpu.HBM)
    rows, keep = RB * len(items), RB * len(kept)
    return pl.pallas_call(
        functools.partial(first_kernel, items, kept),
        in_specs=[hbm] * 5,
        out_specs=[vmem] * (len(items) + 2),
        out_shape=[jax.ShapeDtypeStruct((HALF, K), F32)] * len(items)
        + [
            jax.ShapeDtypeStruct((keep, SLOTS, T, T), BF16),
            jax.ShapeDtypeStruct(sketch.shape, BF16),
        ],
        scratch_shapes=[pltpu.VMEM((rows, SLOTS, T, T), BF16)]
        + [pltpu.SMEM(a.shape, a.dtype) for a in meta]
        + [
            pltpu.SemaphoreType.DMA((3,)),
            pltpu.SemaphoreType.DMA((rows,)),
            pltpu.SemaphoreType.DMA((keep,)),
            pltpu.SemaphoreType.DMA((SKETCH_PIECES,)),
        ],
        compiler_params=pltpu.CompilerParams(vmem_limit_bytes=VMEM_LIMIT),
        cost_estimate=pl.CostEstimate(
            flops=2 * len(items) * HALF * SLOTS * T * K, bytes_accessed=8 << 20, transcendentals=0
        ),
        name="first",
    )(*meta, tiles, sketch)


def spmm_kernel(items, at, loads, joins, cols, counts, scales, tiles, sketch, *refs):
    n = len(items)
    me = lax.axis_index("col")
    adds, outs = refs[:joins], refs[joins:joins + n]
    held, copies = tiles, []
    if loads:
        held, sem = refs[joins + n:]
        copies = tile_copies(me, loads, counts, tiles, held, sem)
    start_all(copies)
    first_ones = RB * n * (SLOTS // 2)
    wait_all(copies[:first_ones])
    for i, item in enumerate(items):
        base = first_row(me, item)
        for r in range(RB):
            to = (at + i) * RB + r
            acc = block_row(base + r, lambda s: held[to, s], cols, counts, scales, sketch)
            rows = slice(r * T, (r + 1) * T)
            for j in range(i, joins, n):
                acc = acc + adds[j][rows, :]
            outs[i][rows, :] = acc
    wait_all(copies[first_ones:])


def spmm(items, at, meta, tiles, sketch, adds=(), loads=()):
    vmem = pl.BlockSpec(memory_space=pltpu.VMEM)
    smem = pl.BlockSpec(memory_space=pltpu.SMEM)
    hbm = pl.BlockSpec(memory_space=pltpu.HBM)
    keep = RB * len(loads)
    out_shape = [jax.ShapeDtypeStruct((HALF, K), F32)] * len(items)
    scratch = []
    if loads:
        out_shape.append(jax.ShapeDtypeStruct((keep, SLOTS, T, T), BF16))
        scratch.append(pltpu.SemaphoreType.DMA((keep,)))
    return pl.pallas_call(
        functools.partial(spmm_kernel, items, at, loads, len(adds)),
        in_specs=[smem] * 3 + [hbm if loads else vmem, vmem] + [vmem] * len(adds),
        out_specs=[vmem] * len(out_shape),
        out_shape=out_shape,
        scratch_shapes=scratch,
        compiler_params=pltpu.CompilerParams(vmem_limit_bytes=VMEM_LIMIT),
        cost_estimate=pl.CostEstimate(
            flops=2 * len(items) * HALF * SLOTS * T * K, bytes_accessed=4 << 20, transcendentals=0
        ),
        name="spmm",
    )(*meta, tiles, sketch, *adds)


PACK = 272
PH = PACK // 2


def gram_kernel(s0, s1, vp, um, up, vm, prod, keep, send, acc, pack):
    chunk = 256
    core = lax.axis_index("col") & 1
    for j in range(1024 // chunk):
        h, o = divmod(j * chunk, HALF)
        rows = slice(o, o + chunk)
        first, second = ((vp, um), (up, vm))[h]
        p = (s0, s1)[h][rows, :] + (first[rows, :] + second[rows, :])
        prod[j * chunk:(j + 1) * chunk, :] = p
        hi, lo = split(p)
        main = dot(hi, hi, ((0,), (0,)))
        cross = dot(hi, lo, ((0,), (0,)))
        if j == 0:
            acc[0] = main
            acc[1] = cross
        else:
            acc[0] += main
            acc[1] += cross
    g = acc[0] + (acc[1] + acc[1].T)
    low = g[T:, T:]
    r = lax.broadcasted_iota(jnp.int32, (T, T), 0)
    c = lax.broadcasted_iota(jnp.int32, (T, T), 1)
    pack[0:T, :] = jnp.where(r >= c, g[:T, :T], low)
    pack[T:K, :] = g[T:, :T]
    diag = jnp.sum(jnp.where(r == c, low, 0.0), axis=0, keepdims=True)
    pack[K:PACK, :] = jnp.broadcast_to(diag, (PACK - K, T))

    @pl.when(core == 0)
    def _():
        keep[...] = pack[:PH, :]
        send[...] = pack[PH:, :]

    @pl.when(core == 1)
    def _():
        keep[...] = pack[PH:, :]
        send[...] = pack[:PH, :]


def gram(s0, s1, vp, um, up, vm):
    vmem = pl.BlockSpec(memory_space=pltpu.VMEM)
    return pl.pallas_call(
        gram_kernel,
        in_specs=[vmem] * 6,
        out_specs=[vmem] * 3,
        scratch_shapes=[pltpu.VMEM((2, K, K), F32), pltpu.VMEM((PACK, T), F32)],
        out_shape=[jax.ShapeDtypeStruct((2 * HALF, K), F32)]
        + [jax.ShapeDtypeStruct((PH, T), F32)] * 2,
        compiler_params=pltpu.CompilerParams(vmem_limit_bytes=VMEM_LIMIT),
        name="gram",
    )(s0, s1, vp, um, up, vm)


def basis_kernel(
    root, mine, other, prod, basis, rfac, pack, a_ref, w_ref, e_ref, r_ref, out, out_sem, r_sem
):
    core = lax.axis_index("col") & 1

    @pl.when(core == 0)
    def _():
        pack[:PH, :] = mine[...]
        pack[PH:, :] = other[...]

    @pl.when(core == 1)
    def _():
        pack[:PH, :] = other[...]
        pack[PH:, :] = mine[...]

    r = lax.broadcasted_iota(jnp.int32, (T, T), 0)
    c = lax.broadcasted_iota(jnp.int32, (T, T), 1)
    m = pack[0:T, :]
    mt = m.T
    b = pack[T:K, :]
    a_ref[:T, :T] = jnp.where(r >= c, m, mt)
    a_ref[T:, :T] = b
    a_ref[:T, T:] = b.T
    a_ref[T:, T:] = jnp.where(r < c, m, jnp.where(r > c, mt, pack[K:K + 1, :]))

    rr = lax.broadcasted_iota(jnp.int32, (K, K), 0)
    cc = lax.broadcasted_iota(jnp.int32, (K, K), 1)
    eye = rr == cc
    a = a_ref[...]
    masked = jnp.where(eye, a, 0.0)
    dcol = lax.rsqrt(jnp.sum(masked, axis=1, keepdims=True))
    drow = lax.rsqrt(jnp.sum(masked, axis=0, keepdims=True))
    unit = jnp.where(eye, 0.0, a * dcol * drow)

    def size(e):
        return jnp.sum(jnp.sum(e * e, axis=0, keepdims=True))

    def lower(e):
        return jnp.where(rr > cc, e, jnp.where(eye, 0.5 * e, 0.0))

    def update(e):
        phi = lower(e).astype(BF16)
        w = w_ref[...]
        t = dot(phi, w.astype(BF16))
        return w - t + dot(phi, t.astype(BF16))

    phi = lower(unit)
    half = phi.astype(BF16)
    w_ref[...] = jnp.where(eye, 1.0, 0.0) - phi + dot(half, half)

    def residual():
        w = w_ref[...]
        t = dot3(w, jnp.where(eye, 1.0, unit))
        e = dot3(t, w, ((1,), (1,))) - jnp.where(eye, 1.0, 0.0)
        e_ref[...] = e
        return size(e)

    def cond(state):
        it, err = state
        return jnp.logical_and(err >= CLOSE, it < 10)

    def body(state):
        it, _ = state
        w_ref[...] = update(e_ref[...])
        return it + 1, residual()

    _, err = lax.while_loop(cond, body, (jnp.int32(0), residual()))
    good = err < CLOSE

    @pl.when(good)
    def _():
        w_ref[...] = update(e_ref[...]) * drow

    @pl.when(jnp.logical_not(good))
    def _():
        w_ref[...] = jnp.where(eye, 1.0, 0.0)
        e_ref[...] = a_ref[...]
        lane = lax.broadcasted_iota(jnp.int32, (1, K), 1)

        def step(k, carry):
            arow = e_ref[pl.ds(k, 1), :]
            wrow = w_ref[pl.ds(k, 1), :]
            inv = lax.rsqrt(jnp.sum(jnp.where(lane == k, arow, 0.0), axis=1, keepdims=True))
            arow = arow * inv
            wrow = wrow * inv
            full = e_ref[...]
            col = jnp.sum(jnp.where(cc == k, full, 0.0), axis=1, keepdims=True) * inv
            col = jnp.where(rr[:, :1] > k, col, 0.0)
            e_ref[...] = full - col * arow
            w_ref[...] = w_ref[...] - col * wrow
            w_ref[pl.ds(k, 1), :] = wrow
            return carry

        lax.fori_loop(0, K, step, 0)

    w = w_ref[...]
    wh, wl = split(w * root)
    dims = ((1,), (1,))
    copies = []
    for j in range(4):
        rows = slice(j * 256, (j + 1) * 256)
        ph, plo = split(prod[rows, :])
        out[rows, :] = dot(ph, wh, dims) + (dot(ph, wl, dims) + dot(plo, wh, dims))
        copies.append(pltpu.make_async_copy(out.at[rows], basis.at[rows], out_sem.at[j]))
        copies[-1].start()
    upper = dot3(w, a_ref[...])
    r_ref[...] = jnp.where(rr <= cc, upper, 0.0) * (1.0 / root)
    copies.append(pltpu.make_async_copy(r_ref, rfac, r_sem))
    copies[-1].start()
    for copy in copies:
        copy.wait()


def finish(root, mine, other, prod):
    vmem = pl.BlockSpec(memory_space=pltpu.VMEM)
    return pl.pallas_call(
        functools.partial(basis_kernel, root),
        in_specs=[vmem] * 3,
        out_specs=[pl.BlockSpec(memory_space=pltpu.HBM)] * 2,
        scratch_shapes=[pltpu.VMEM((PACK, T), F32)]
        + [pltpu.VMEM((K, K), F32)] * 4
        + [
            pltpu.VMEM((2 * HALF, K), F32),
            pltpu.SemaphoreType.DMA((4,)),
            pltpu.SemaphoreType.DMA,
        ],
        out_shape=[
            jax.ShapeDtypeStruct((2 * HALF, K), F32),
            jax.ShapeDtypeStruct((K, K), F32),
        ],
        compiler_params=pltpu.CompilerParams(vmem_limit_bytes=VMEM_LIMIT),
        name="finish",
    )(mine, other, prod)


ORDERS = ((2, 1), (1, 0), (0, 2))


def perm(size, target):
    return [(i, target(i)) for i in range(size)]


def axis_perm(order, by):
    def target(i):
        place = [i >> 5, (i >> 3) & 3, (i >> 1) & 3]
        axis = order[i & 1]
        place[axis] = (place[axis] + by) & 3
        return (((place[0] * 4 + place[1]) * 4 + place[2]) << 1) | (i & 1)

    return perm(128, target)


def on_device(tiles, tile_cols, counts, scales, sketch):
    rows_all = tiles.shape[0] * T * lax.axis_size("row")
    meta = tuple(
        pltpu.with_memory_space_constraint(a, pltpu.HBM) for a in (tile_cols.T, counts.T, scales.T)
    )
    partner = perm(8, lambda c: c ^ 1)
    plus = perm(8, lambda c: (c + 2) % 8)
    minus = perm(8, lambda c: (c + 6) % 8)

    def move(q, to):
        return lax.ppermute(q, "col", to)

    far_other = (2, 1, 0), (2, 1, 1)
    far_own = (2, 0, 0), (2, 0, 1)
    u_other, u_own = ((1, 1, 1), (3, 1, 0)), ((1, 0, 1), (3, 0, 0))
    v_other, v_own = ((1, 1, 0), (3, 1, 1)), ((1, 0, 0), (3, 0, 1))
    here_other, here_own = ((0, 1, 0), (0, 1, 1)), ((0, 0, 0), (0, 0, 1))
    tiles = pltpu.with_memory_space_constraint(tiles, pltpu.HBM)
    sketch = pltpu.with_memory_space_constraint(sketch, pltpu.HBM)

    qa, qb, held, local = first(far_other, far_own, meta, tiles, sketch)

    def sp(items, at, held, **kw):
        return spmm(items, at, meta, held, local, **kw)

    ca, cb = move(qa, partner), move(qb, partner)
    fa, fb = sp(far_own, 0, held)
    tp, tm = move(fa + ca, plus), move(fb + cb, minus)
    rest = u_other + v_other + u_own + here_other + v_own + here_own
    *qu, held = sp(u_other, 0, tiles, loads=rest)
    cu = [move(q, partner) for q in qu]
    qv = sp(v_other, 2, held)
    cv = [move(q, partner) for q in qv]
    up, um = sp(u_own, 4, held, adds=cu)
    up, um = move(up, plus), move(um, minus)
    qo = sp(here_other, 6, held)
    co = [move(q, partner) for q in qo]
    vp, vm = sp(v_own, 8, held, adds=(*cv, tp, tm))
    vp, vm = move(vp, plus), move(vm, minus)
    s0, s1 = sp(here_own, 10, held, adds=co)

    prod, keep, send = gram(s0, s1, vp, um, up, vm)
    tot = keep + move(send, partner)
    both = ("row", "col")
    for order in ORDERS:
        got = [lax.ppermute(tot, both, axis_perm(order, by)) for by in (3, 1, 2)]
        tot = (tot + got[0]) + (got[1] + got[2])
    rest = move(tot, partner)
    basis, rfac = finish(float(rows_all) ** 0.5, tot, rest, prod)
    return basis, rfac


def solution(mesh):
    in_specs = (
        P("row", "col", None, None),
        P("row", "col"),
        P("row", "col"),
        P("row", "col"),
        P("col", None),
    )
    out_specs = (P(("row", "col"), None), P())

    return jax.shard_map(
        on_device, mesh=mesh, in_specs=in_specs, out_specs=out_specs, check_vma=False
    )
```

```python
import functools

import jax
import jax.numpy as jnp
from jax import lax
from jax.experimental import pallas as pl
from jax.experimental.pallas import tpu as pltpu
from jax.sharding import PartitionSpec as P


F32 = jnp.float32
BF16 = jnp.bfloat16
RB = 4
SLOTS = 8
T = 128
K = 256
HALF = RB * T
VMEM_LIMIT = 16 << 20
SKETCH_PIECES = 4
CLOSE = 4e-3


def split(a):
    hi = a.astype(BF16)
    return hi, (a - hi.astype(F32)).astype(BF16)


def dot(a, b, dims=((1,), (0,))):
    return lax.dot_general(a, b, (dims, ((), ())), preferred_element_type=F32)


def dot3(a, b, dims=((1,), (0,))):
    ah, al = a if isinstance(a, tuple) else split(a)
    bh, bl = b if isinstance(b, tuple) else split(b)
    (ca,), (cb,) = dims
    return dot(jnp.concatenate([ah, ah, al], ca), jnp.concatenate([bh, bl, bh], cb), dims)


def first_row(me, item):
    dx, flip, half = item
    return ((((me >> 1) + dx) & 3) * 2 + ((me + flip) & 1)) * 2 * RB + half * RB


def block_row(row, tile, cols, counts, scales, sketch):
    live = counts[0, row]
    dense = []
    blocks = []
    for s in range(SLOTS):
        scaled = jnp.where(s < live, tile(s).astype(F32) * scales[s, row], 0.0)
        dense.append(scaled.astype(BF16))
        start = pl.multiple_of(cols[s, row] * T, T)
        blocks.append(sketch[pl.ds(start, T), :])
    return dot(jnp.concatenate(dense, axis=1), jnp.concatenate(blocks, axis=0))


def tile_copies(me, items, counts, tiles, into, sem):
    copies = []
    for i, item in enumerate(items):
        for r in range(RB):
            row = first_row(me, item) + r
            pairs = (counts[0, row] + 1) >> 1
            at = i * RB + r
            for p in range(1, SLOTS // 2 + 1):
                part = pl.ds(0, 2 * p)
                copy = pltpu.make_async_copy(tiles.at[row, part], into.at[at, part], sem.at[at])
                copies.append((pairs == p, copy))
    return copies


def start_all(copies):
    for chosen, copy in copies:
        pl.when(chosen)(copy.start)


def wait_all(copies):
    for chosen, copy in copies:
        pl.when(chosen)(copy.wait)


def first_kernel(items, kept, cols, counts, scales, tiles, sketch, *refs):
    n = len(items)
    outs, (held, local) = refs[:n], refs[n:n + 2]
    buf, meta, meta_sem, tile_sem, held_sem, sketch_sem = (
        refs[n + 2], refs[n + 3:n + 6], *refs[n + 6:]
    )
    me = lax.axis_index("col")
    piece = local.shape[0] // SKETCH_PIECES
    load = [
        pltpu.make_async_copy(src, dst, meta_sem.at[i])
        for i, (src, dst) in enumerate(zip((cols, counts, scales), meta))
    ]
    for j in range(SKETCH_PIECES):
        rows = pl.ds(j * piece, piece)
        load.append(pltpu.make_async_copy(sketch.at[rows], local.at[rows], sketch_sem.at[j]))
    for copy in load:
        copy.start()
    for copy in load[:3]:
        copy.wait()
    mine = tile_copies(me, items, meta[1], tiles, buf, tile_sem)
    later = tile_copies(me, kept, meta[1], tiles, held, held_sem)
    start_all(mine)
    start_all(later)
    for copy in load[3:]:
        copy.wait()
    wait_all(mine)
    for i, item in enumerate(items):
        base = first_row(me, item)
        for r in range(RB):
            outs[i][r * T:(r + 1) * T, :] = block_row(
                base + r, lambda s: buf[i * RB + r, s], *meta, local
            )
    wait_all(later)


def first(items, kept, meta, tiles, sketch):
    vmem = pl.BlockSpec(memory_space=pltpu.VMEM)
    hbm = pl.BlockSpec(memory_space=pltpu.HBM)
    rows, keep = RB * len(items), RB * len(kept)
    return pl.pallas_call(
        functools.partial(first_kernel, items, kept),
        in_specs=[hbm] * 5,
        out_specs=[vmem] * (len(items) + 2),
        out_shape=[jax.ShapeDtypeStruct((HALF, K), F32)] * len(items)
        + [
            jax.ShapeDtypeStruct((keep, SLOTS, T, T), BF16),
            jax.ShapeDtypeStruct(sketch.shape, BF16),
        ],
        scratch_shapes=[pltpu.VMEM((rows, SLOTS, T, T), BF16)]
        + [pltpu.SMEM(a.shape, a.dtype) for a in meta]
        + [
            pltpu.SemaphoreType.DMA((3,)),
            pltpu.SemaphoreType.DMA((rows,)),
            pltpu.SemaphoreType.DMA((keep,)),
            pltpu.SemaphoreType.DMA((SKETCH_PIECES,)),
        ],
        compiler_params=pltpu.CompilerParams(vmem_limit_bytes=VMEM_LIMIT),
        cost_estimate=pl.CostEstimate(
            flops=2 * len(items) * HALF * SLOTS * T * K, bytes_accessed=8 << 20, transcendentals=0
        ),
        name="first",
    )(*meta, tiles, sketch)


def spmm_kernel(items, at, loads, joins, cols, counts, scales, tiles, sketch, *refs):
    n = len(items)
    me = lax.axis_index("col")
    adds, outs = refs[:joins], refs[joins:joins + n]
    held, copies = tiles, []
    if loads:
        held, sem = refs[joins + n:]
        copies = tile_copies(me, loads, counts, tiles, held, sem)
    start_all(copies)
    first_ones = RB * n * (SLOTS // 2)
    wait_all(copies[:first_ones])
    for i, item in enumerate(items):
        base = first_row(me, item)
        for r in range(RB):
            to = (at + i) * RB + r
            acc = block_row(base + r, lambda s: held[to, s], cols, counts, scales, sketch)
            rows = slice(r * T, (r + 1) * T)
            for j in range(i, joins, n):
                acc = acc + adds[j][rows, :]
            outs[i][rows, :] = acc
    wait_all(copies[first_ones:])


def spmm(items, at, meta, tiles, sketch, adds=(), loads=()):
    vmem = pl.BlockSpec(memory_space=pltpu.VMEM)
    smem = pl.BlockSpec(memory_space=pltpu.SMEM)
    hbm = pl.BlockSpec(memory_space=pltpu.HBM)
    keep = RB * len(loads)
    out_shape = [jax.ShapeDtypeStruct((HALF, K), F32)] * len(items)
    scratch = []
    if loads:
        out_shape.append(jax.ShapeDtypeStruct((keep, SLOTS, T, T), BF16))
        scratch.append(pltpu.SemaphoreType.DMA((keep,)))
    return pl.pallas_call(
        functools.partial(spmm_kernel, items, at, loads, len(adds)),
        in_specs=[smem] * 3 + [hbm if loads else vmem, vmem] + [vmem] * len(adds),
        out_specs=[vmem] * len(out_shape),
        out_shape=out_shape,
        scratch_shapes=scratch,
        compiler_params=pltpu.CompilerParams(vmem_limit_bytes=VMEM_LIMIT),
        cost_estimate=pl.CostEstimate(
            flops=2 * len(items) * HALF * SLOTS * T * K, bytes_accessed=4 << 20, transcendentals=0
        ),
        name="spmm",
    )(*meta, tiles, sketch, *adds)


PACK = 272
PH = PACK // 2


def gram_kernel(s0, s1, vp, um, up, vm, prod, keep, send, acc, pack):
    chunk = 256
    core = lax.axis_index("col") & 1
    for j in range(1024 // chunk):
        h, o = divmod(j * chunk, HALF)
        rows = slice(o, o + chunk)
        first, second = ((vp, um), (up, vm))[h]
        p = (s0, s1)[h][rows, :] + (first[rows, :] + second[rows, :])
        prod[j * chunk:(j + 1) * chunk, :] = p
        hi, lo = split(p)
        both = dot(hi, jnp.concatenate([hi, lo], axis=1), ((0,), (0,)))
        if j == 0:
            acc[...] = both
        else:
            acc[...] += both
    cross = acc[:, K:]
    g = acc[:, :K] + (cross + cross.T)
    low = g[T:, T:]
    r = lax.broadcasted_iota(jnp.int32, (T, T), 0)
    c = lax.broadcasted_iota(jnp.int32, (T, T), 1)
    pack[0:T, :] = jnp.where(r >= c, g[:T, :T], low)
    pack[T:K, :] = g[T:, :T]
    diag = jnp.sum(jnp.where(r == c, low, 0.0), axis=0, keepdims=True)
    pack[K:PACK, :] = jnp.broadcast_to(diag, (PACK - K, T))

    @pl.when(core == 0)
    def _():
        keep[...] = pack[:PH, :]
        send[...] = pack[PH:, :]

    @pl.when(core == 1)
    def _():
        keep[...] = pack[PH:, :]
        send[...] = pack[:PH, :]


def gram(s0, s1, vp, um, up, vm):
    vmem = pl.BlockSpec(memory_space=pltpu.VMEM)
    return pl.pallas_call(
        gram_kernel,
        in_specs=[vmem] * 6,
        out_specs=[vmem] * 3,
        scratch_shapes=[pltpu.VMEM((K, 2 * K), F32), pltpu.VMEM((PACK, T), F32)],
        out_shape=[jax.ShapeDtypeStruct((2 * HALF, K), F32)]
        + [jax.ShapeDtypeStruct((PH, T), F32)] * 2,
        compiler_params=pltpu.CompilerParams(vmem_limit_bytes=VMEM_LIMIT),
        name="gram",
    )(s0, s1, vp, um, up, vm)


def basis_kernel(
    root, mine, other, prod, basis, rfac, pack, a_ref, w_ref, e_ref, r_ref, out, out_sem, r_sem
):
    core = lax.axis_index("col") & 1

    @pl.when(core == 0)
    def _():
        pack[:PH, :] = mine[...]
        pack[PH:, :] = other[...]

    @pl.when(core == 1)
    def _():
        pack[:PH, :] = other[...]
        pack[PH:, :] = mine[...]

    r = lax.broadcasted_iota(jnp.int32, (T, T), 0)
    c = lax.broadcasted_iota(jnp.int32, (T, T), 1)
    m = pack[0:T, :]
    mt = m.T
    b = pack[T:K, :]
    a_ref[:T, :T] = jnp.where(r >= c, m, mt)
    a_ref[T:, :T] = b
    a_ref[:T, T:] = b.T
    a_ref[T:, T:] = jnp.where(r < c, m, jnp.where(r > c, mt, pack[K:K + 1, :]))

    rr = lax.broadcasted_iota(jnp.int32, (K, K), 0)
    cc = lax.broadcasted_iota(jnp.int32, (K, K), 1)
    eye = rr == cc
    a = a_ref[...]
    masked = jnp.where(eye, a, 0.0)
    dcol = lax.rsqrt(jnp.sum(masked, axis=1, keepdims=True))
    drow = lax.rsqrt(jnp.sum(masked, axis=0, keepdims=True))
    unit = jnp.where(eye, 0.0, a * dcol * drow)

    def size(e):
        return jnp.sum(jnp.sum(e * e, axis=0, keepdims=True))

    def lower(e):
        return jnp.where(rr > cc, e, jnp.where(eye, 0.5 * e, 0.0))

    def change(e):
        p = lower(e)
        h = p.astype(BF16)
        return dot(h, h) + lower(dot(h, h, ((1,), (1,)))) - p

    def update(e):
        w = w_ref[...]
        return w + dot(change(e).astype(BF16), w.astype(BF16))

    w_ref[...] = jnp.where(eye, 1.0, 0.0) + change(unit)

    def residual():
        w = w_ref[...]
        t = dot3(w, jnp.where(eye, 1.0, unit))
        e = dot3(t, w, ((1,), (1,))) - jnp.where(eye, 1.0, 0.0)
        e_ref[...] = e
        return size(e)

    def cond(state):
        it, err = state
        return jnp.logical_and(err >= CLOSE, it < 10)

    def body(state):
        it, _ = state
        w_ref[...] = update(e_ref[...])
        return it + 1, residual()

    _, err = lax.while_loop(cond, body, (jnp.int32(0), residual()))
    good = err < CLOSE

    @pl.when(good)
    def _():
        w_ref[...] = update(e_ref[...]) * drow

    @pl.when(jnp.logical_not(good))
    def _():
        w_ref[...] = jnp.where(eye, 1.0, 0.0)
        e_ref[...] = a_ref[...]
        lane = lax.broadcasted_iota(jnp.int32, (1, K), 1)

        def step(k, carry):
            arow = e_ref[pl.ds(k, 1), :]
            wrow = w_ref[pl.ds(k, 1), :]
            inv = lax.rsqrt(jnp.sum(jnp.where(lane == k, arow, 0.0), axis=1, keepdims=True))
            arow = arow * inv
            wrow = wrow * inv
            full = e_ref[...]
            col = jnp.sum(jnp.where(cc == k, full, 0.0), axis=1, keepdims=True) * inv
            col = jnp.where(rr[:, :1] > k, col, 0.0)
            e_ref[...] = full - col * arow
            w_ref[...] = w_ref[...] - col * wrow
            w_ref[pl.ds(k, 1), :] = wrow
            return carry

        lax.fori_loop(0, K, step, 0)

    w = w_ref[...]
    scaled = split(w * root)
    copies = []
    for j in range(4):
        rows = slice(j * 256, (j + 1) * 256)
        out[rows, :] = dot3(prod[rows, :], scaled, ((1,), (1,)))
        copies.append(pltpu.make_async_copy(out.at[rows], basis.at[rows], out_sem.at[j]))
        copies[-1].start()
    upper = dot3(w, a_ref[...])
    r_ref[...] = jnp.where(rr <= cc, upper, 0.0) * (1.0 / root)
    copies.append(pltpu.make_async_copy(r_ref, rfac, r_sem))
    copies[-1].start()
    for copy in copies:
        copy.wait()


def finish(root, mine, other, prod):
    vmem = pl.BlockSpec(memory_space=pltpu.VMEM)
    return pl.pallas_call(
        functools.partial(basis_kernel, root),
        in_specs=[vmem] * 3,
        out_specs=[pl.BlockSpec(memory_space=pltpu.HBM)] * 2,
        scratch_shapes=[pltpu.VMEM((PACK, T), F32)]
        + [pltpu.VMEM((K, K), F32)] * 4
        + [
            pltpu.VMEM((2 * HALF, K), F32),
            pltpu.SemaphoreType.DMA((4,)),
            pltpu.SemaphoreType.DMA,
        ],
        out_shape=[
            jax.ShapeDtypeStruct((2 * HALF, K), F32),
            jax.ShapeDtypeStruct((K, K), F32),
        ],
        compiler_params=pltpu.CompilerParams(vmem_limit_bytes=VMEM_LIMIT),
        name="finish",
    )(mine, other, prod)


ORDERS = ((0, 1), (1, 2), (2, 0))


def perm(size, target):
    return [(i, target(i)) for i in range(size)]


def axis_perm(order, by):
    def target(i):
        place = [i >> 5, (i >> 3) & 3, (i >> 1) & 3]
        axis = order[i & 1]
        place[axis] = (place[axis] + by) & 3
        return (((place[0] * 4 + place[1]) * 4 + place[2]) << 1) | (i & 1)

    return perm(128, target)


def on_device(tiles, tile_cols, counts, scales, sketch):
    rows_all = tiles.shape[0] * T * lax.axis_size("row")
    meta = tuple(
        pltpu.with_memory_space_constraint(a, pltpu.HBM) for a in (tile_cols.T, counts.T, scales.T)
    )
    partner = perm(8, lambda c: c ^ 1)
    plus = perm(8, lambda c: (c + 2) % 8)
    minus = perm(8, lambda c: (c + 6) % 8)

    def move(q, to):
        return lax.ppermute(q, "col", to)

    far_other = (2, 1, 0), (2, 1, 1)
    far_own = (2, 0, 0), (2, 0, 1)
    u_other, u_own = ((1, 1, 1), (3, 1, 0)), ((1, 0, 1), (3, 0, 0))
    v_other, v_own = ((1, 1, 0), (3, 1, 1)), ((1, 0, 0), (3, 0, 1))
    here_other, here_own = ((0, 1, 0), (0, 1, 1)), ((0, 0, 0), (0, 0, 1))
    tiles = pltpu.with_memory_space_constraint(tiles, pltpu.HBM)
    sketch = pltpu.with_memory_space_constraint(sketch, pltpu.HBM)

    qa, qb, held, local = first(far_other, far_own, meta, tiles, sketch)

    def sp(items, at, held, **kw):
        return spmm(items, at, meta, held, local, **kw)

    ca, cb = move(qa, partner), move(qb, partner)
    fa, fb = sp(far_own, 0, held)
    tp, tm = move(fa + ca, plus), move(fb + cb, minus)
    *qu, held = sp(u_other, 0, tiles, loads=u_other + u_own)
    cu = [move(q, partner) for q in qu]
    fu = sp(u_own, 2, held)
    up, um = move(fu[0] + cu[0], plus), move(fu[1] + cu[1], minus)
    *qv, held = sp(v_other, 0, tiles, loads=v_other + v_own + here_other + here_own)
    cv = [move(q, partner) for q in qv]
    qo = sp(here_other, 4, held)
    co = [move(q, partner) for q in qo]
    vp, vm = sp(v_own, 2, held, adds=(*cv, tp, tm))
    vp, vm = move(vp, plus), move(vm, minus)
    s0, s1 = sp(here_own, 6, held, adds=co)

    prod, keep, send = gram(s0, s1, vp, um, up, vm)
    tot = keep + move(send, partner)
    both = ("row", "col")
    for order in ORDERS:
        got = [lax.ppermute(tot, both, axis_perm(order, by)) for by in (3, 1, 2)]
        tot = (tot + got[0]) + (got[1] + got[2])
    rest = move(tot, partner)
    basis, rfac = finish(float(rows_all) ** 0.5, tot, rest, prod)
    return basis, rfac


def solution(mesh):
    in_specs = (
        P("row", "col", None, None),
        P("row", "col"),
        P("row", "col"),
        P("row", "col"),
        P("col", None),
    )
    out_specs = (P(("row", "col"), None), P())

    return jax.shard_map(
        on_device, mesh=mesh, in_specs=in_specs, out_specs=out_specs, check_vma=False
    )
```
